32 devices in a mesh: energy: 8 (over y, x, core), cuts: 4 (over z).
Axes of the slice: x: 2, y: 2, z: 4, core: 2. Of those that a mesh axis runs over, the one named last changes fastest.
Arguments:
- green_diag: bfloat16 [4, 32, 2, 256, 256], P('cuts', 'energy'), may hold values from -0.375 to 0.375
- green_upper: bfloat16 [4, 32, 2, 256, 256], P('cuts', 'energy'), may hold values from -0.375 to 0.375
- sigma_lesser: bfloat16 [4, 32, 2, 256, 256], P('cuts', 'energy'), may hold values from -6 to 6
- screening: bfloat16 [4, 32, 2, 256, 256], P('cuts', 'energy'), may hold values from -0.375 to 0.375
Outputs:
- polar_screened: bfloat16 [4, 32, 2, 256, 256], P('cuts', 'energy')
The draws below stay inside these ranges and needn't reach their ends.
All inputs are finite; a program needn't handle non-finite values.
Results may differ from the reference program's by a relative error of at most 0.013.
Values may be sent and summed in bfloat16 or wider, within the bound.
A program may use at most 64 MiB of HBM per device.

```python
import jax
import jax.numpy as jnp
from jax import lax

B = 256
NE = 32
SLICES = 4
PAD = 64


def shard_levels(own_key, dims, cuts, least, top_value):
    def one(dim, blocks):
        steps = jax.random.uniform(jax.random.fold_in(jax.random.fold_in(own_key, 6), dim), (blocks,), jnp.float32, least / len(cuts), top_value / len(cuts))
        return jnp.repeat(jnp.exp(steps), dims[dim] // blocks).reshape((-1,) + (1,) * (len(dims) - dim - 1))

    loudness = one(*cuts[0])
    for cut in cuts[1:]:
        loudness = loudness * one(*cut)
    return loudness


def centred(rng, extent, spread, most, split=(), dtype=jnp.bfloat16):
    gain = shard_levels(rng, extent, split, -0.22, 0.18) if split else 1.0
    array = jax.random.normal(rng, extent, jnp.float32) * spread * gain
    return jnp.minimum(jnp.maximum(array, -most), most).astype(dtype)


def setup_inputs(seed: int = 0) -> dict:
    arg_keys = jax.random.split(jax.random.key(seed), 5)
    return {
        "green_diag": centred(arg_keys[0], (SLICES, NE, 2, B, B), B ** -0.5, 0.375, ((0, 4), (1, 8))),
        "green_upper": centred(arg_keys[1], (SLICES, NE, 2, B, B), B ** -0.5, 0.375, ((0, 4), (1, 8))),
        "sigma_lesser": centred(arg_keys[2], (SLICES, NE, 2, B, B), 1.0, 6.0, ((0, 4), (1, 8))),
        "screening": centred(arg_keys[3], (SLICES, NE, 2, B, B), B ** -0.5, 0.375, ((0, 4), (1, 8))),
    }


def times_block(left, right):
    left = left.astype(jnp.float32)
    right = right.astype(jnp.float32)
    real = jnp.einsum('eij,ejk->eik', left[:, 0], right[:, 0]) - jnp.einsum('eij,ejk->eik', left[:, 1], right[:, 1])
    imag = jnp.einsum('eij,ejk->eik', left[:, 0], right[:, 1]) + jnp.einsum('eij,ejk->eik', left[:, 1], right[:, 0])
    return jnp.stack([real, imag], axis=1)


def times_adjoint(left, right):
    left = left.astype(jnp.float32)
    right = right.astype(jnp.float32)
    real = jnp.einsum('eij,ekj->eik', left[:, 0], right[:, 0]) + jnp.einsum('eij,ekj->eik', left[:, 1], right[:, 1])
    imag = jnp.einsum('eij,ekj->eik', left[:, 1], right[:, 0]) - jnp.einsum('eij,ekj->eik', left[:, 0], right[:, 1])
    return jnp.stack([real, imag], axis=1)


def one_slice(inputs):
    green_diag, green_upper, sigma_here, sigma_after, screening = inputs
    own_term = times_block(green_diag, sigma_here).astype(jnp.bfloat16)
    pair_term = times_block(green_upper, sigma_after).astype(jnp.bfloat16)
    lesser = (times_adjoint(own_term, green_diag) + times_adjoint(pair_term, green_upper)).astype(jnp.bfloat16)
    values = lesser.astype(jnp.float32)
    signal = lax.complex(values[:, 0], values[:, 1])
    spectrum = jnp.fft.fft(signal, n=PAD, axis=0)
    power = jnp.real(spectrum) ** 2 + jnp.imag(spectrum) ** 2
    lagged = jnp.fft.ifft(power, axis=0)[:NE]
    polar = (jnp.stack([jnp.real(lagged), jnp.imag(lagged)], axis=1) / NE).astype(jnp.bfloat16)
    screened_left = times_block(screening, polar).astype(jnp.bfloat16)
    return times_adjoint(screened_left, screening).astype(jnp.bfloat16)


def reference(green_diag, green_upper, sigma_lesser, screening):
    sigma_next = jnp.concatenate([sigma_lesser[1:], jnp.zeros_like(sigma_lesser[:1])], axis=0)
    return lax.map(one_slice, (green_diag, green_upper, sigma_lesser, sigma_next, screening))
```

```python
import functools

import jax
import jax.numpy as jnp
import numpy as np
from jax import lax
from jax.experimental import pallas as pl
from jax.experimental.pallas import tpu as pltpu
from jax.sharding import PartitionSpec as P

LANES = 128
MESH = pl.DeviceIdType.MESH
F32 = jnp.float32
BF16 = jnp.bfloat16


def tables(groups, local):
    energies = groups * local
    period = 2 * energies
    order = np.array([s * local + j for j in range(local) for s in range(groups)])
    freq = np.arange(period)
    angle = 2.0 * np.pi * ((freq[:, None] * order[None, :]) % period) / period
    cos, sin = np.cos(angle), np.sin(angle)
    forward = np.zeros((2 * period, energies, 2))
    forward[:period, :, 0], forward[:period, :, 1] = cos, sin
    forward[period:, :, 0], forward[period:, :, 1] = -sin, cos
    forward = forward.reshape(2 * period, 2 * energies).astype(np.float32)
    inverse = np.stack([cos.T, sin.T], axis=1).reshape(2 * energies, period)
    inverse = (inverse / (period * energies)).astype(np.float32)

    def split(table):
        high = table.astype(BF16)
        return high, (table - high.astype(np.float32)).astype(BF16)

    f_high, f_low = split(forward)
    i_high, i_low = split(inverse)
    return (
        np.concatenate([f_high, f_low], axis=1),
        np.concatenate([i_high, i_high, i_low], axis=1),
    )


def dot(left, right):
    return jnp.dot(left, right, preferred_element_type=F32)


def dot_t(left, right):
    return lax.dot_general(left, right, (((1,), (1,)), ((), ())), preferred_element_type=F32)


def times(lr, li, rr, ri):
    return dot(lr, rr) - dot(li, ri), dot(lr, ri) + dot(li, rr)


def times_adjoint(lr, li, rr, ri):
    return dot_t(lr, rr) + dot_t(li, ri), dot_t(li, rr) - dot_t(lr, ri)


def kernel(
    groups, slices, halves,
    gd_hbm, gu_hbm, s_hbm, w_hbm, fwd_ref, inv_ref, out_hbm,
    gd, gu, sig, scr, snext, own, lbuf, entries, xf, pf, pbuf, back, obuf,
    in_sem, z_send, z_recv, a_send, a_recv, b_send, b_recv, o_sem,
):
    me = lax.axis_index("energy")
    cut = lax.axis_index("cuts")
    local, _, size, _ = gd.shape
    rows = size // groups
    part = rows // halves
    count = 2 * groups * local
    slab = 2 * groups * rows

    barrier = pltpu.get_barrier_semaphore()

    def greet(k, carry):
        pl.semaphore_signal(
            barrier, inc=1, device_id={"energy": lax.rem(me + k, groups)}, device_id_type=MESH
        )
        return carry

    @pl.when(cut > 0)
    def _():
        pl.semaphore_signal(barrier, inc=1, device_id={"cuts": cut - 1}, device_id_type=MESH)

    @pl.when(cut < slices - 1)
    def _():
        pl.semaphore_signal(barrier, inc=1, device_id={"cuts": cut + 1}, device_id_type=MESH)

    lax.fori_loop(1, groups, greet, 0)

    loads = [
        pltpu.make_async_copy(source, target, in_sem.at[i])
        for i, (source, target) in enumerate(
            [(gd_hbm, gd), (s_hbm, sig), (gu_hbm, gu), (w_hbm, scr)]
        )
    ]
    loads[0].start()
    loads[1].start()

    edges = jnp.where(cut > 0, 1, 0) + jnp.where(cut < slices - 1, 1, 0)
    pl.semaphore_wait(barrier, groups - 1 + edges)

    def shift(j):
        return pltpu.make_async_remote_copy(
            src_ref=s_hbm.at[j], dst_ref=snext.at[j],
            send_sem=z_send.at[j], recv_sem=z_recv.at[j],
            device_id={"cuts": cut - 1}, device_id_type=MESH,
        )

    @pl.when(cut > 0)
    def _():
        for j in range(local):
            shift(j).start()

    loads[2].start()
    loads[3].start()
    loads[0].wait()
    loads[1].wait()

    def own_step(j, carry):
        tr, ti = times(gd[j, 0], gd[j, 1], sig[j, 0], sig[j, 1])
        lr, li = times_adjoint(tr.astype(BF16), ti.astype(BF16), gd[j, 0], gd[j, 1])
        own[j, 0] = lr
        own[j, 1] = li
        return carry

    lax.fori_loop(0, local, own_step, 0)
    loads[2].wait()
    loads[3].wait()

    def take(j):
        pltpu.make_async_copy(
            entries.at[j, pl.ds(0, groups - 1)], entries.at[j, pl.ds(0, groups - 1)], a_recv.at[j]
        ).wait()
        wide = entries[j].astype(F32).reshape(slab, size)
        for q in range(size // LANES):
            xf[pl.ds(q * count * rows + j * slab, slab), :] = wide[:, q * LANES : (q + 1) * LANES]

    def lesser_step(j, carry):
        @pl.when(cut < slices - 1)
        def _():
            shift(j).wait_recv()
            tr, ti = times(gu[j, 0], gu[j, 1], snext[j, 0], snext[j, 1])
            lr, li = times_adjoint(tr.astype(BF16), ti.astype(BF16), gu[j, 0], gu[j, 1])
            own[j, 0] += lr
            own[j, 1] += li

        for c in range(2):
            value = own[j, c].astype(BF16).reshape(groups, rows, size)
            lbuf[j, :, c] = value
        entries[j, me] = lbuf[j, me]

        def send(k, inner):
            to = lax.rem(me + k, groups)
            pltpu.make_async_remote_copy(
                src_ref=lbuf.at[j, to], dst_ref=entries.at[j, me],
                send_sem=a_send.at[j], recv_sem=a_recv.at[j],
                device_id={"energy": to}, device_id_type=MESH,
            ).start()
            return inner

        lax.fori_loop(1, groups, send, 0)

        @pl.when(j > 0)
        def _():
            take(j - 1)

        return carry

    lax.fori_loop(0, local, lesser_step, 0)
    take(local - 1)

    period = count

    for h in range(halves):

        def correlate(i, carry):
            r = h * part + i
            x = jnp.concatenate(
                [xf[pl.ds(q * count * rows + r, count, stride=rows), :] for q in range(size // LANES)],
                axis=1,
            ).astype(BF16)
            spec = dot(fwd_ref[...], jnp.concatenate([x, x], axis=0))
            re, im = spec[:period], spec[period:]
            power = re * re + im * im
            high = power.astype(BF16)
            low = (power - high.astype(F32)).astype(BF16)
            lag = dot(inv_ref[...], jnp.concatenate([high, low, high], axis=0))
            for q in range(size // LANES):
                pf[pl.ds(q * count * rows + r, count, stride=rows), :] = lag[:, q * LANES : (q + 1) * LANES]
            return carry

        lax.fori_loop(0, part, correlate, 0, unroll=4)

        def ship(j, carry):
            lags = jnp.concatenate(
                [pf[pl.ds(q * count * rows + j * slab, slab), :] for q in range(size // LANES)], axis=1
            )
            lags = lags.reshape(groups, 2, rows, size)[:, :, h * part : (h + 1) * part]
            pbuf[h, j] = lags.astype(BF16)
            back[j, me, h] = pbuf[h, j, me]

            def send(k, inner):
                to = lax.rem(me + k, groups)
                pltpu.make_async_remote_copy(
                    src_ref=pbuf.at[h, j, to], dst_ref=back.at[j, me, h],
                    send_sem=b_send.at[h, j], recv_sem=b_recv.at[h, j],
                    device_id={"energy": to}, device_id_type=MESH,
                ).start()
                return inner

            lax.fori_loop(1, groups, send, 0)
            return carry

        lax.fori_loop(0, local, ship, 0)

    def result_step(j, carry):
        for h in range(halves):
            landed = back.at[j, pl.ds(0, groups - 1), h]
            pltpu.make_async_copy(landed, landed, b_recv.at[h, j]).wait()
        pr = back[j, :, :, 0].reshape(size, size)
        pi = back[j, :, :, 1].reshape(size, size)
        tr, ti = times(scr[j, 0], scr[j, 1], pr, pi)
        lr, li = times_adjoint(tr.astype(BF16), ti.astype(BF16), scr[j, 0], scr[j, 1])
        obuf[j, 0] = lr.astype(BF16)
        obuf[j, 1] = li.astype(BF16)
        pltpu.make_async_copy(obuf.at[j], out_hbm.at[j], o_sem.at[j]).start()
        return carry

    lax.fori_loop(0, local, result_step, 0)

    @pl.when(cut > 0)
    def _():
        for j in range(local):
            shift(j).wait_send()

    for j in range(local):
        sent = lbuf.at[j, pl.ds(0, groups - 1)]
        pltpu.make_async_copy(sent, sent, a_send.at[j]).wait()
        for h in range(halves):
            sent = pbuf.at[h, j, pl.ds(0, groups - 1)]
            pltpu.make_async_copy(sent, sent, b_send.at[h, j]).wait()
        pltpu.make_async_copy(obuf.at[j], out_hbm.at[j], o_sem.at[j]).wait()


def solution(mesh):
    groups, slices = mesh.shape["energy"], mesh.shape["cuts"]

    def shards(green_diag, green_upper, sigma_lesser, screening):
        shape = green_diag.shape[1:]
        local, _, size, _ = shape
        rows = size // groups
        halves = max(1, rows // 16)
        part = rows // halves
        count = 2 * groups * local
        forward, inverse = tables(groups, local)
        block = pltpu.VMEM(shape, BF16)
        dma = pltpu.SemaphoreType.DMA
        anywhere = pl.BlockSpec(memory_space=pl.ANY)
        vmem = pl.BlockSpec(memory_space=pltpu.VMEM)
        result = pl.pallas_call(
            functools.partial(kernel, groups, slices, halves),
            out_shape=jax.ShapeDtypeStruct(shape, BF16),
            in_specs=[anywhere] * 4 + [vmem] * 2,
            out_specs=anywhere,
            scratch_shapes=[
                block, block, block, block, block,
                pltpu.VMEM(shape, F32),
                pltpu.VMEM((local, groups, 2, rows, size), BF16),
                pltpu.VMEM((local, groups, 2, rows, size), BF16),
                pltpu.VMEM((size // LANES * count * rows, LANES), F32),
                pltpu.VMEM((size // LANES * count * rows, LANES), F32),
                pltpu.VMEM((halves, local, groups, 2, part, size), BF16),
                pltpu.VMEM((local, groups, halves, 2, part, size), BF16),
                block,
                dma((4,)),
                dma((local,)), dma((local,)),
                dma((local,)), dma((local,)),
                dma((halves, local)), dma((halves, local)),
                dma((local,)),
            ],
            compiler_params=pltpu.CompilerParams(
                collective_id=0, has_side_effects=True, vmem_limit_bytes=48 * 1024 * 1024
            ),
        )(
            green_diag[0], green_upper[0], sigma_lesser[0], screening[0],
            jnp.asarray(forward), jnp.asarray(inverse),
        )
        return result[None]

    spec = P("cuts", "energy", None, None, None)
    return jax.shard_map(
        shards, mesh=mesh, in_specs=(spec,) * 4, out_specs=spec, check_vma=False
    )
```

```python
import functools

import jax
import jax.numpy as jnp
import numpy as np
from jax import lax
from jax.experimental import pallas as pl
from jax.experimental.pallas import tpu as pltpu
from jax.sharding import PartitionSpec as P

LANES = 128
MESH = pl.DeviceIdType.MESH
F32 = jnp.float32
BF16 = jnp.bfloat16


def tables(groups, local):
    energies = groups * local
    period = 2 * energies
    order = np.array([s * local + j for j in range(local) for s in range(groups)])
    freq = np.arange(period)
    angle = 2.0 * np.pi * ((freq[:, None] * order[None, :]) % period) / period
    cos, sin = np.cos(angle), np.sin(angle)
    forward = np.zeros((2 * period, energies, 2))
    forward[:period, :, 0], forward[:period, :, 1] = cos, sin
    forward[period:, :, 0], forward[period:, :, 1] = -sin, cos
    forward = forward.reshape(2 * period, 2 * energies).astype(np.float32)
    inverse = np.stack([cos.T, sin.T], axis=1).reshape(2 * energies, period)
    inverse = (inverse / (period * energies)).astype(np.float32)

    def split(table):
        high = table.astype(BF16)
        return high, (table - high.astype(np.float32)).astype(BF16)

    f_high, f_low = split(forward)
    i_high, i_low = split(inverse)
    return (
        np.concatenate([f_high, f_low], axis=1),
        np.concatenate([i_high, i_high, i_low], axis=1),
    )


def dot(left, right):
    return jnp.dot(left, right, preferred_element_type=F32)


def dot_t(left, right):
    return lax.dot_general(left, right, (((1,), (1,)), ((), ())), preferred_element_type=F32)


def times(lr, li, rr, ri):
    return dot(lr, rr) - dot(li, ri), dot(lr, ri) + dot(li, rr)


def times_adjoint(lr, li, rr, ri):
    return dot_t(lr, rr) + dot_t(li, ri), dot_t(li, rr) - dot_t(lr, ri)


def kernel(
    groups, slices, halves,
    gd_hbm, gu_hbm, s_hbm, w_hbm, fwd_hbm, inv_hbm, out_hbm,
    fwd_ref, inv_ref,    gd, gu, sig, scr, snext, own, lbuf, entries, xf, pf, pbuf, back, obuf,
    in_sem, z_send, z_recv, a_send, a_recv, b_send, b_recv, o_sem,
):
    me = lax.axis_index("energy")
    cut = lax.axis_index("cuts")
    local, _, size, _ = gd.shape
    rows = size // groups
    part = rows // halves
    count = 2 * groups * local
    slab = 2 * groups * rows

    barrier = pltpu.get_barrier_semaphore()

    def greet(k, carry):
        pl.semaphore_signal(
            barrier, inc=1, device_id={"energy": lax.rem(me + k, groups)}, device_id_type=MESH
        )
        return carry

    @pl.when(cut > 0)
    def _():
        pl.semaphore_signal(barrier, inc=1, device_id={"cuts": cut - 1}, device_id_type=MESH)

    @pl.when(cut < slices - 1)
    def _():
        pl.semaphore_signal(barrier, inc=1, device_id={"cuts": cut + 1}, device_id_type=MESH)

    lax.fori_loop(1, groups, greet, 0)

    loads = [
        pltpu.make_async_copy(source, target, in_sem.at[i])
        for i, (source, target) in enumerate(
            [(gd_hbm, gd), (s_hbm, sig), (gu_hbm, gu), (w_hbm, scr), (fwd_hbm, fwd_ref), (inv_hbm, inv_ref)]
        )
    ]
    loads[0].start()
    loads[1].start()

    edges = jnp.where(cut > 0, 1, 0) + jnp.where(cut < slices - 1, 1, 0)
    pl.semaphore_wait(barrier, groups - 1 + edges)

    def shift(j):
        return pltpu.make_async_remote_copy(
            src_ref=s_hbm.at[j], dst_ref=snext.at[j],
            send_sem=z_send.at[j], recv_sem=z_recv.at[j],
            device_id={"cuts": cut - 1}, device_id_type=MESH,
        )

    @pl.when(cut > 0)
    def _():
        for j in range(local):
            shift(j).start()

    for load in loads[2:]:
        load.start()
    loads[0].wait()
    loads[1].wait()

    def own_step(j, carry):
        tr, ti = times(gd[j, 0], gd[j, 1], sig[j, 0], sig[j, 1])
        lr, li = times_adjoint(tr.astype(BF16), ti.astype(BF16), gd[j, 0], gd[j, 1])
        own[j, 0] = lr
        own[j, 1] = li
        return carry

    lax.fori_loop(0, local, own_step, 0)
    for load in loads[2:]:
        load.wait()

    def take(j):
        pltpu.make_async_copy(
            entries.at[j, pl.ds(0, groups - 1)], entries.at[j, pl.ds(0, groups - 1)], a_recv.at[j]
        ).wait()
        wide = entries[j].astype(F32).reshape(slab, size)
        for q in range(size // LANES):
            xf[pl.ds(q * count * rows + j * slab, slab), :] = wide[:, q * LANES : (q + 1) * LANES]

    def lesser_step(j, carry):
        @pl.when(cut < slices - 1)
        def _():
            shift(j).wait_recv()
            tr, ti = times(gu[j, 0], gu[j, 1], snext[j, 0], snext[j, 1])
            lr, li = times_adjoint(tr.astype(BF16), ti.astype(BF16), gu[j, 0], gu[j, 1])
            own[j, 0] += lr
            own[j, 1] += li

        for c in range(2):
            value = own[j, c].astype(BF16).reshape(groups, rows, size)
            lbuf[j, :, c] = value
        entries[j, me] = lbuf[j, me]

        def send(k, inner):
            to = lax.rem(me + k, groups)
            pltpu.make_async_remote_copy(
                src_ref=lbuf.at[j, to], dst_ref=entries.at[j, me],
                send_sem=a_send.at[j], recv_sem=a_recv.at[j],
                device_id={"energy": to}, device_id_type=MESH,
            ).start()
            return inner

        lax.fori_loop(1, groups, send, 0)

        @pl.when(j > 0)
        def _():
            take(j - 1)

        return carry

    lax.fori_loop(0, local, lesser_step, 0)
    take(local - 1)

    period = count

    for h in range(halves):

        def correlate(i, carry):
            r = h * part + i
            x = jnp.concatenate(
                [xf[pl.ds(q * count * rows + r, count, stride=rows), :] for q in range(size // LANES)],
                axis=1,
            ).astype(BF16)
            spec = dot(fwd_ref[...], jnp.concatenate([x, x], axis=0))
            re, im = spec[:period], spec[period:]
            power = re * re + im * im
            high = power.astype(BF16)
            low = (power - high.astype(F32)).astype(BF16)
            lag = dot(inv_ref[...], jnp.concatenate([high, low, high], axis=0))
            for q in range(size // LANES):
                pf[pl.ds(q * count * rows + r, count, stride=rows), :] = lag[:, q * LANES : (q + 1) * LANES]
            return carry

        lax.fori_loop(0, part, correlate, 0, unroll=4)

        def ship(j, carry):
            lags = jnp.concatenate(
                [pf[pl.ds(q * count * rows + j * slab, slab), :] for q in range(size // LANES)], axis=1
            )
            lags = lags.reshape(groups, 2, rows, size)[:, :, h * part : (h + 1) * part]
            pbuf[h, j] = lags.astype(BF16)
            back[j, me, h] = pbuf[h, j, me]

            def send(k, inner):
                to = lax.rem(me + k, groups)
                pltpu.make_async_remote_copy(
                    src_ref=pbuf.at[h, j, to], dst_ref=back.at[j, me, h],
                    send_sem=b_send.at[h, j], recv_sem=b_recv.at[h, j],
                    device_id={"energy": to}, device_id_type=MESH,
                ).start()
                return inner

            lax.fori_loop(1, groups, send, 0)
            return carry

        lax.fori_loop(0, local, ship, 0)

    def result_step(j, carry):
        for h in range(halves):
            landed = back.at[j, pl.ds(0, groups - 1), h]
            pltpu.make_async_copy(landed, landed, b_recv.at[h, j]).wait()
        pr = back[j, :, :, 0].reshape(size, size)
        pi = back[j, :, :, 1].reshape(size, size)
        tr, ti = times(scr[j, 0], scr[j, 1], pr, pi)
        lr, li = times_adjoint(tr.astype(BF16), ti.astype(BF16), scr[j, 0], scr[j, 1])
        obuf[j, 0] = lr.astype(BF16)
        obuf[j, 1] = li.astype(BF16)
        pltpu.make_async_copy(obuf.at[j], out_hbm.at[j], o_sem.at[j]).start()
        return carry

    lax.fori_loop(0, local, result_step, 0)

    @pl.when(cut > 0)
    def _():
        for j in range(local):
            shift(j).wait_send()

    for j in range(local):
        sent = lbuf.at[j, pl.ds(0, groups - 1)]
        pltpu.make_async_copy(sent, sent, a_send.at[j]).wait()
        for h in range(halves):
            sent = pbuf.at[h, j, pl.ds(0, groups - 1)]
            pltpu.make_async_copy(sent, sent, b_send.at[h, j]).wait()
        pltpu.make_async_copy(obuf.at[j], out_hbm.at[j], o_sem.at[j]).wait()


def solution(mesh):
    groups, slices = mesh.shape["energy"], mesh.shape["cuts"]

    def shards(green_diag, green_upper, sigma_lesser, screening):
        shape = green_diag.shape[1:]
        local, _, size, _ = shape
        rows = size // groups
        halves = max(1, rows // 16)
        part = rows // halves
        count = 2 * groups * local
        forward, inverse = tables(groups, local)
        block = pltpu.VMEM(shape, BF16)
        dma = pltpu.SemaphoreType.DMA
        anywhere = pl.BlockSpec(memory_space=pltpu.HBM)
        result = pl.pallas_call(
            functools.partial(kernel, groups, slices, halves),
            out_shape=jax.ShapeDtypeStruct(shape, BF16),
            in_specs=[anywhere] * 6,
            out_specs=anywhere,
            scratch_shapes=[
                pltpu.VMEM(forward.shape, BF16),
                pltpu.VMEM(inverse.shape, BF16),
                block, block, block, block, block,
                pltpu.VMEM(shape, F32),
                pltpu.VMEM((local, groups, 2, rows, size), BF16),
                pltpu.VMEM((local, groups, 2, rows, size), BF16),
                pltpu.VMEM((size // LANES * count * rows, LANES), F32),
                pltpu.VMEM((size // LANES * count * rows, LANES), F32),
                pltpu.VMEM((halves, local, groups, 2, part, size), BF16),
                pltpu.VMEM((local, groups, halves, 2, part, size), BF16),
                block,
                dma((6,)),
                dma((local,)), dma((local,)),
                dma((local,)), dma((local,)),
                dma((halves, local)), dma((halves, local)),
                dma((local,)),
            ],
            compiler_params=pltpu.CompilerParams(
                collective_id=0, has_side_effects=True, vmem_limit_bytes=60 * 1024 * 1024
            ),
        )(
            green_diag[0], green_upper[0], sigma_lesser[0], screening[0],
            jnp.asarray(forward), jnp.asarray(inverse),
        )
        return result[None]

    spec = P("cuts", "energy", None, None, None)
    return jax.shard_map(
        shards, mesh=mesh, in_specs=(spec,) * 4, out_specs=spec, check_vma=False
    )
```

```python
import functools

import jax
import jax.numpy as jnp
import numpy as np
from jax import lax
from jax.experimental import pallas as pl
from jax.experimental.pallas import tpu as pltpu
from jax.sharding import PartitionSpec as P

LANES = 128
MESH = pl.DeviceIdType.MESH
F32 = jnp.float32
BF16 = jnp.bfloat16


def tables(groups, local):
    energies = groups * local
    period = 2 * energies
    order = np.array([s * local + j for j in range(local) for s in range(groups)])
    freq = np.arange(period)
    angle = 2.0 * np.pi * ((freq[:, None] * order[None, :]) % period) / period
    cos, sin = np.cos(angle), np.sin(angle)
    forward = np.zeros((2 * period, energies, 2))
    forward[:period, :, 0], forward[:period, :, 1] = cos, sin
    forward[period:, :, 0], forward[period:, :, 1] = -sin, cos
    forward = forward.reshape(2 * period, 2 * energies).astype(np.float32)
    inverse = np.stack([cos.T, sin.T], axis=1).reshape(2 * energies, period)
    inverse = (inverse / (period * energies)).astype(np.float32)

    def split(table):
        high = table.astype(BF16)
        return high, (table - high.astype(np.float32)).astype(BF16)

    f_high, f_low = split(forward)
    i_high, i_low = split(inverse)
    return (
        np.concatenate([f_high, f_low], axis=1),
        np.concatenate([i_high, i_high, i_low], axis=1),
    )


def dot(left, right):
    return jnp.dot(left, right, preferred_element_type=F32)


def dot_t(left, right):
    return lax.dot_general(left, right, (((1,), (1,)), ((), ())), preferred_element_type=F32)


def times(lr, li, rr, ri):
    return dot(lr, rr) - dot(li, ri), dot(lr, ri) + dot(li, rr)


def times_adjoint(lr, li, rr, ri):
    return dot_t(lr, rr) + dot_t(li, ri), dot_t(li, rr) - dot_t(lr, ri)


def kernel(
    groups, slices, parts,
    gd_hbm, gu_hbm, s_hbm, w_hbm, fwd_hbm, inv_hbm, out_hbm,
    fwd_ref, inv_ref,    gd, gu, sig, scr, snext, own, lbuf, entries, xf, pf, pbuf, back, obuf,
    in_sem, z_send, z_recv, a_send, a_recv, b_send, b_recv, o_sem,
):
    me = lax.axis_index("energy")
    cut = lax.axis_index("cuts")
    local, _, size, _ = gd.shape
    rows = size // groups
    part = rows // parts
    count = 2 * groups * local

    barrier = pltpu.get_barrier_semaphore()

    def greet(k, carry):
        pl.semaphore_signal(
            barrier, inc=1, device_id={"energy": lax.rem(me + k, groups)}, device_id_type=MESH
        )
        return carry

    @pl.when(cut > 0)
    def _():
        pl.semaphore_signal(barrier, inc=1, device_id={"cuts": cut - 1}, device_id_type=MESH)

    @pl.when(cut < slices - 1)
    def _():
        pl.semaphore_signal(barrier, inc=1, device_id={"cuts": cut + 1}, device_id_type=MESH)

    lax.fori_loop(1, groups, greet, 0)

    loads = [
        pltpu.make_async_copy(source, target, in_sem.at[i])
        for i, (source, target) in enumerate(
            [(gd_hbm, gd), (s_hbm, sig), (gu_hbm, gu), (w_hbm, scr), (fwd_hbm, fwd_ref), (inv_hbm, inv_ref)]
        )
    ]
    loads[0].start()
    loads[1].start()

    edges = jnp.where(cut > 0, 1, 0) + jnp.where(cut < slices - 1, 1, 0)
    pl.semaphore_wait(barrier, groups - 1 + edges)

    def shift(j):
        return pltpu.make_async_remote_copy(
            src_ref=s_hbm.at[j], dst_ref=snext.at[j],
            send_sem=z_send.at[j], recv_sem=z_recv.at[j],
            device_id={"cuts": cut - 1}, device_id_type=MESH,
        )

    @pl.when(cut > 0)
    def _():
        for j in range(local):
            shift(j).start()

    for load in loads[2:]:
        load.start()
    loads[0].wait()
    loads[1].wait()

    def own_step(j, carry):
        tr, ti = times(gd[j, 0], gd[j, 1], sig[j, 0], sig[j, 1])
        lr, li = times_adjoint(tr.astype(BF16), ti.astype(BF16), gd[j, 0], gd[j, 1])
        own[j, 0] = lr
        own[j, 1] = li
        return carry

    lax.fori_loop(0, local, own_step, 0)
    for load in loads[2:]:
        load.wait()

    stretch = 2 * groups * part

    def take(j, h):
        landed = entries.at[j, h, pl.ds(0, groups - 1)]
        pltpu.make_async_copy(landed, landed, a_recv.at[j, h]).wait()
        wide = entries[j, h].astype(F32).reshape(stretch, size)
        for q in range(size // LANES):
            at = q * count * rows + h * count * part + j * stretch
            xf[pl.ds(at, stretch), :] = wide[:, q * LANES : (q + 1) * LANES]

    def each_part(body):
        lax.fori_loop(0, parts, lambda h, carry: (body(h), carry)[1], 0)

    def lesser_step(j, carry):
        @pl.when(cut < slices - 1)
        def _():
            shift(j).wait_recv()
            tr, ti = times(gu[j, 0], gu[j, 1], snext[j, 0], snext[j, 1])
            lr, li = times_adjoint(tr.astype(BF16), ti.astype(BF16), gu[j, 0], gu[j, 1])
            own[j, 0] += lr
            own[j, 1] += li

        for c in range(2):
            value = own[j, c].astype(BF16).reshape(groups, parts, part, size)
            for h in range(parts):
                lbuf[j, h, :, c] = value[:, h]

        def spread(h):
            def send(k, inner):
                to = lax.rem(me + k, groups)
                pltpu.make_async_remote_copy(
                    src_ref=lbuf.at[j, h, to], dst_ref=entries.at[j, h, me],
                    send_sem=a_send.at[j, h], recv_sem=a_recv.at[j, h],
                    device_id={"energy": to}, device_id_type=MESH,
                ).start()
                return inner

            lax.fori_loop(1, groups, send, 0)
            entries[j, h, me] = lbuf[j, h, me]

        each_part(spread)

        @pl.when(j > 0)
        def _():
            each_part(lambda h: take(j - 1, h))

        return carry

    lax.fori_loop(0, local, lesser_step, 0)

    period = count

    def part_step(h, outer):
        take(local - 1, h)

        def correlate(i, carry):
            at = h * count * part + i
            x = jnp.concatenate(
                [xf[pl.ds(q * count * rows + at, count, stride=part), :] for q in range(size // LANES)],
                axis=1,
            ).astype(BF16)
            spec = dot(fwd_ref[...], jnp.concatenate([x, x], axis=0))
            re, im = spec[:period], spec[period:]
            power = re * re + im * im
            high = power.astype(BF16)
            low = (power - high.astype(F32)).astype(BF16)
            lag = dot(inv_ref[...], jnp.concatenate([high, low, high], axis=0))
            for q in range(size // LANES):
                pf[pl.ds(q * count * rows + at, count, stride=part), :] = (
                    lag[:, q * LANES : (q + 1) * LANES]
                )
            return carry

        lax.fori_loop(0, part, correlate, 0, unroll=min(part, 4))

        def ship(j, carry):
            lags = jnp.concatenate(
                [
                    pf[pl.ds(q * count * rows + h * count * part + j * stretch, stretch), :]
                    for q in range(size // LANES)
                ],
                axis=1,
            )
            pbuf[h, j] = lags.reshape(groups, 2, part, size).astype(BF16)

            def send(k, inner):
                to = lax.rem(me + k, groups)
                pltpu.make_async_remote_copy(
                    src_ref=pbuf.at[h, j, to], dst_ref=back.at[j, h, me],
                    send_sem=b_send.at[h, j], recv_sem=b_recv.at[h, j],
                    device_id={"energy": to}, device_id_type=MESH,
                ).start()
                return inner

            lax.fori_loop(1, groups, send, 0)
            back[j, h, me] = pbuf[h, j, me]
            return carry

        lax.fori_loop(0, local, ship, 0)
        return outer

    lax.fori_loop(0, parts, part_step, 0)

    def result_step(j, carry):
        for h in range(parts):
            landed = back.at[j, h, pl.ds(0, groups - 1)]
            pltpu.make_async_copy(landed, landed, b_recv.at[h, j]).wait()
        pr, pi = (
            jnp.stack([back[j, h, :, c] for h in range(parts)], axis=1).reshape(size, size)
            for c in range(2)
        )
        tr, ti = times(scr[j, 0], scr[j, 1], pr, pi)
        lr, li = times_adjoint(tr.astype(BF16), ti.astype(BF16), scr[j, 0], scr[j, 1])
        obuf[j, 0] = lr.astype(BF16)
        obuf[j, 1] = li.astype(BF16)
        pltpu.make_async_copy(obuf.at[j], out_hbm.at[j], o_sem.at[j]).start()
        return carry

    lax.fori_loop(0, local, result_step, 0)

    @pl.when(cut > 0)
    def _():
        for j in range(local):
            shift(j).wait_send()

    for j in range(local):
        for h in range(parts):
            sent = lbuf.at[j, h, pl.ds(0, groups - 1)]
            pltpu.make_async_copy(sent, sent, a_send.at[j, h]).wait()
            sent = pbuf.at[h, j, pl.ds(0, groups - 1)]
            pltpu.make_async_copy(sent, sent, b_send.at[h, j]).wait()
        pltpu.make_async_copy(obuf.at[j], out_hbm.at[j], o_sem.at[j]).wait()


def solution(mesh):
    groups, slices = mesh.shape["energy"], mesh.shape["cuts"]

    def shards(green_diag, green_upper, sigma_lesser, screening):
        shape = green_diag.shape[1:]
        local, _, size, _ = shape
        rows = size // groups
        parts = max(1, rows // 8)
        part = rows // parts
        count = 2 * groups * local
        forward, inverse = tables(groups, local)
        block = pltpu.VMEM(shape, BF16)
        dma = pltpu.SemaphoreType.DMA
        anywhere = pl.BlockSpec(memory_space=pltpu.HBM)
        result = pl.pallas_call(
            functools.partial(kernel, groups, slices, parts),
            out_shape=jax.ShapeDtypeStruct(shape, BF16),
            in_specs=[anywhere] * 6,
            out_specs=anywhere,
            scratch_shapes=[
                pltpu.VMEM(forward.shape, BF16),
                pltpu.VMEM(inverse.shape, BF16),
                block, block, block, block, block,
                pltpu.VMEM(shape, F32),
                pltpu.VMEM((local, parts, groups, 2, part, size), BF16),
                pltpu.VMEM((local, parts, groups, 2, part, size), BF16),
                pltpu.VMEM((size // LANES * count * rows, LANES), F32),
                pltpu.VMEM((size // LANES * count * rows, LANES), F32),
                pltpu.VMEM((parts, local, groups, 2, part, size), BF16),
                pltpu.VMEM((local, parts, groups, 2, part, size), BF16),
                block,
                dma((6,)),
                dma((local,)), dma((local,)),
                dma((local, parts)), dma((local, parts)),
                dma((parts, local)), dma((parts, local)),
                dma((local,)),
            ],
            compiler_params=pltpu.CompilerParams(
                collective_id=0, has_side_effects=True, vmem_limit_bytes=60 * 1024 * 1024
            ),
        )(
            green_diag[0], green_upper[0], sigma_lesser[0], screening[0],
            jnp.asarray(forward), jnp.asarray(inverse),
        )
        return result[None]

    spec = P("cuts", "energy", None, None, None)
    return jax.shard_map(
        shards, mesh=mesh, in_specs=(spec,) * 4, out_specs=spec, check_vma=False
    )
```

```python
import functools

import jax
import jax.numpy as jnp
import numpy as np
from jax import lax
from jax.experimental import pallas as pl
from jax.experimental.pallas import tpu as pltpu
from jax.sharding import PartitionSpec as P

LANES = 128
MESH = pl.DeviceIdType.MESH
F32 = jnp.float32
BF16 = jnp.bfloat16


def tables(groups, local):
    energies = groups * local
    period = 2 * energies
    order = np.array([s * local + j for j in range(local) for s in range(groups)])
    freq = np.arange(period)
    angle = 2.0 * np.pi * ((freq[:, None] * order[None, :]) % period) / period
    cos, sin = np.cos(angle), np.sin(angle)
    forward = np.zeros((2 * period, energies, 2))
    forward[:period, :, 0], forward[:period, :, 1] = cos, sin
    forward[period:, :, 0], forward[period:, :, 1] = -sin, cos
    forward = forward.reshape(2 * period, 2 * energies).astype(np.float32)
    inverse = np.stack([cos.T, sin.T], axis=1).reshape(2 * energies, period)
    inverse = (inverse / (period * energies)).astype(np.float32)

    def split(table):
        high = table.astype(BF16)
        return high, (table - high.astype(np.float32)).astype(BF16)

    f_high, f_low = split(forward)
    i_high, i_low = split(inverse)
    return (
        np.concatenate([f_high, f_low], axis=1),
        np.concatenate([i_high, i_high, i_low], axis=1),
    )


def dot(left, right):
    return jnp.dot(left, right, preferred_element_type=F32)


def dot_t(left, right):
    return lax.dot_general(left, right, (((1,), (1,)), ((), ())), preferred_element_type=F32)


def times(lr, li, rr, ri):
    return dot(lr, rr) - dot(li, ri), dot(lr, ri) + dot(li, rr)


def times_adjoint(lr, li, rr, ri):
    return dot_t(lr, rr) + dot_t(li, ri), dot_t(li, rr) - dot_t(lr, ri)


def kernel(
    groups, slices, parts,
    gd_hbm, gu_hbm, s_hbm, w_hbm, fwd_hbm, inv_hbm, out_hbm,
    fwd_ref, inv_ref,    gd, gu, sig, scr, snext, loan, own, lbuf, entries, xf, pf, pbuf, back, obuf,
    in_sem, z_send, z_recv, l_sem, a_send, a_recv, b_send, b_recv, o_sem,
):
    me = lax.axis_index("energy")
    cut = lax.axis_index("cuts")
    local, _, size, _ = gd.shape
    rows = size // groups
    part = rows // parts
    count = 2 * groups * local

    barrier = pltpu.get_barrier_semaphore()

    first = lax.rem(me, 2)
    partner = me + 1 - 2 * first
    last = local - 1

    def greet(k, carry):
        pl.semaphore_signal(
            barrier, inc=1, device_id={"energy": lax.rem(me + k, groups)}, device_id_type=MESH
        )
        return carry

    @pl.when(cut > 0)
    def _():
        for who in (me, partner):
            pl.semaphore_signal(
                barrier, inc=1, device_id={"energy": who, "cuts": cut - 1}, device_id_type=MESH
            )

    @pl.when(cut < slices - 1)
    def _():
        for who in (me, partner):
            pl.semaphore_signal(
                barrier, inc=1, device_id={"energy": who, "cuts": cut + 1}, device_id_type=MESH
            )

    lax.fori_loop(1, groups, greet, 0)

    loads = [
        pltpu.make_async_copy(source, target, in_sem.at[i])
        for i, (source, target) in enumerate(
            [(gd_hbm, gd), (s_hbm, sig), (gu_hbm, gu), (w_hbm, scr), (fwd_hbm, fwd_ref), (inv_hbm, inv_ref)]
        )
    ]
    loads[0].start()
    loads[1].start()

    edges = jnp.where(cut > 0, 1, 0) + jnp.where(cut < slices - 1, 1, 0)
    pl.semaphore_wait(barrier, groups - 1 + 2 * edges)

    def shift(j):
        return pltpu.make_async_remote_copy(
            src_ref=s_hbm.at[j], dst_ref=snext.at[j],
            send_sem=z_send.at[j], recv_sem=z_recv.at[j],
            device_id={"energy": me, "cuts": cut - 1}, device_id_type=MESH,
        )

    def lend():
        return pltpu.make_async_remote_copy(
            src_ref=s_hbm.at[last, 1 - first], dst_ref=loan,
            send_sem=l_sem.at[0], recv_sem=l_sem.at[1],
            device_id={"energy": partner, "cuts": cut}, device_id_type=MESH,
        )

    def shift_mine():
        return pltpu.make_async_remote_copy(
            src_ref=s_hbm.at[last, first], dst_ref=snext.at[last, first],
            send_sem=z_send.at[last], recv_sem=z_recv.at[last],
            device_id={"energy": me, "cuts": cut - 1}, device_id_type=MESH,
        )

    def shift_loan():
        return pltpu.make_async_remote_copy(
            src_ref=loan, dst_ref=snext.at[last, first],
            send_sem=z_send.at[local], recv_sem=z_recv.at[local],
            device_id={"energy": partner, "cuts": cut - 1}, device_id_type=MESH,
        )

    @pl.when(cut > 0)
    def _():
        lend().start()
        for j in range(last):
            shift(j).start()
        lend().wait_recv()

        @pl.when(first == 0)
        def _():
            shift_mine().start()
            shift_loan().start()

        @pl.when(first == 1)
        def _():
            shift_loan().start()
            shift_mine().start()

    for load in loads[2:]:
        load.start()
    loads[0].wait()
    loads[1].wait()

    def own_step(j, carry):
        tr, ti = times(gd[j, 0], gd[j, 1], sig[j, 0], sig[j, 1])
        lr, li = times_adjoint(tr.astype(BF16), ti.astype(BF16), gd[j, 0], gd[j, 1])
        own[j, 0] = lr
        own[j, 1] = li
        return carry

    lax.fori_loop(0, local, own_step, 0)
    for load in loads[2:]:
        load.wait()

    stretch = 2 * groups * part

    def take(j, h):
        landed = entries.at[j, h, pl.ds(0, groups - 1)]
        pltpu.make_async_copy(landed, landed, a_recv.at[j, h]).wait()
        wide = entries[j, h].astype(F32).reshape(stretch, size)
        for q in range(size // LANES):
            at = q * count * rows + h * count * part + j * stretch
            xf[pl.ds(at, stretch), :] = wide[:, q * LANES : (q + 1) * LANES]

    def each_part(body):
        lax.fori_loop(0, parts, lambda h, carry: (body(h), carry)[1], 0)

    def lesser_step(j, carry):
        @pl.when(cut < slices - 1)
        def _():
            @pl.when(j < last)
            def _():
                shift(j).wait_recv()

            @pl.when(j == last)
            def _():
                shift_mine().wait_recv()
                shift_loan().wait_recv()

            tr, ti = times(gu[j, 0], gu[j, 1], snext[j, 0], snext[j, 1])
            lr, li = times_adjoint(tr.astype(BF16), ti.astype(BF16), gu[j, 0], gu[j, 1])
            own[j, 0] += lr
            own[j, 1] += li

        for c in range(2):
            value = own[j, c].astype(BF16).reshape(groups, parts, part, size)
            for h in range(parts):
                lbuf[j, h, :, c] = value[:, h]

        def spread(h):
            def send(k, inner):
                to = lax.rem(me + k, groups)
                pltpu.make_async_remote_copy(
                    src_ref=lbuf.at[j, h, to], dst_ref=entries.at[j, h, me],
                    send_sem=a_send.at[j, h], recv_sem=a_recv.at[j, h],
                    device_id={"energy": to}, device_id_type=MESH,
                ).start()
                return inner

            lax.fori_loop(1, groups, send, 0)
            entries[j, h, me] = lbuf[j, h, me]

        each_part(spread)

        @pl.when(j > 0)
        def _():
            each_part(lambda h: take(j - 1, h))

        return carry

    lax.fori_loop(0, local, lesser_step, 0)

    period = count

    def part_step(h, outer):
        take(local - 1, h)

        def correlate(i, carry):
            at = h * count * part + i
            x = jnp.concatenate(
                [xf[pl.ds(q * count * rows + at, count, stride=part), :] for q in range(size // LANES)],
                axis=1,
            ).astype(BF16)
            spec = dot(fwd_ref[...], jnp.concatenate([x, x], axis=0))
            re, im = spec[:period], spec[period:]
            power = re * re + im * im
            high = power.astype(BF16)
            low = (power - high.astype(F32)).astype(BF16)
            lag = dot(inv_ref[...], jnp.concatenate([high, low, high], axis=0))
            for q in range(size // LANES):
                pf[pl.ds(q * count * rows + at, count, stride=part), :] = (
                    lag[:, q * LANES : (q + 1) * LANES]
                )
            return carry

        lax.fori_loop(0, part, correlate, 0, unroll=min(part, 4))

        def ship(j, carry):
            lags = jnp.concatenate(
                [
                    pf[pl.ds(q * count * rows + h * count * part + j * stretch, stretch), :]
                    for q in range(size // LANES)
                ],
                axis=1,
            )
            pbuf[h, j] = lags.reshape(groups, 2, part, size).astype(BF16)

            def send(k, inner):
                to = lax.rem(me + k, groups)
                pltpu.make_async_remote_copy(
                    src_ref=pbuf.at[h, j, to], dst_ref=back.at[j, h, me],
                    send_sem=b_send.at[h, j], recv_sem=b_recv.at[h, j],
                    device_id={"energy": to}, device_id_type=MESH,
                ).start()
                return inner

            lax.fori_loop(1, groups, send, 0)
            back[j, h, me] = pbuf[h, j, me]
            return carry

        lax.fori_loop(0, local, ship, 0)
        return outer

    lax.fori_loop(0, parts, part_step, 0)

    def result_step(j, carry):
        for h in range(parts):
            landed = back.at[j, h, pl.ds(0, groups - 1)]
            pltpu.make_async_copy(landed, landed, b_recv.at[h, j]).wait()
        pr, pi = (
            jnp.stack([back[j, h, :, c] for h in range(parts)], axis=1).reshape(size, size)
            for c in range(2)
        )
        tr, ti = times(scr[j, 0], scr[j, 1], pr, pi)
        lr, li = times_adjoint(tr.astype(BF16), ti.astype(BF16), scr[j, 0], scr[j, 1])
        obuf[j, 0] = lr.astype(BF16)
        obuf[j, 1] = li.astype(BF16)
        pltpu.make_async_copy(obuf.at[j], out_hbm.at[j], o_sem.at[j]).start()
        return carry

    lax.fori_loop(0, local, result_step, 0)

    @pl.when(cut > 0)
    def _():
        for j in range(last):
            shift(j).wait_send()
        shift_mine().wait_send()
        shift_loan().wait_send()
        lend().wait_send()

    for j in range(local):
        for h in range(parts):
            sent = lbuf.at[j, h, pl.ds(0, groups - 1)]
            pltpu.make_async_copy(sent, sent, a_send.at[j, h]).wait()
            sent = pbuf.at[h, j, pl.ds(0, groups - 1)]
            pltpu.make_async_copy(sent, sent, b_send.at[h, j]).wait()
        pltpu.make_async_copy(obuf.at[j], out_hbm.at[j], o_sem.at[j]).wait()


def solution(mesh):
    groups, slices = mesh.shape["energy"], mesh.shape["cuts"]

    def shards(green_diag, green_upper, sigma_lesser, screening):
        shape = green_diag.shape[1:]
        local, _, size, _ = shape
        rows = size // groups
        parts = max(1, rows // 8)
        part = rows // parts
        count = 2 * groups * local
        forward, inverse = tables(groups, local)
        block = pltpu.VMEM(shape, BF16)
        dma = pltpu.SemaphoreType.DMA
        anywhere = pl.BlockSpec(memory_space=pltpu.HBM)
        result = pl.pallas_call(
            functools.partial(kernel, groups, slices, parts),
            out_shape=jax.ShapeDtypeStruct(shape, BF16),
            in_specs=[anywhere] * 6,
            out_specs=anywhere,
            scratch_shapes=[
                pltpu.VMEM(forward.shape, BF16),
                pltpu.VMEM(inverse.shape, BF16),
                block, block, block, block, block,
                pltpu.VMEM(shape[2:], BF16),
                pltpu.VMEM(shape, F32),
                pltpu.VMEM((local, parts, groups, 2, part, size), BF16),
                pltpu.VMEM((local, parts, groups, 2, part, size), BF16),
                pltpu.VMEM((size // LANES * count * rows, LANES), F32),
                pltpu.VMEM((size // LANES * count * rows, LANES), F32),
                pltpu.VMEM((parts, local, groups, 2, part, size), BF16),
                pltpu.VMEM((local, parts, groups, 2, part, size), BF16),
                block,
                dma((6,)),
                dma((local + 1,)), dma((local + 1,)), dma((2,)),
                dma((local, parts)), dma((local, parts)),
                dma((parts, local)), dma((parts, local)),
                dma((local,)),
            ],
            compiler_params=pltpu.CompilerParams(
                collective_id=0, has_side_effects=True, vmem_limit_bytes=60 * 1024 * 1024
            ),
        )(
            green_diag[0], green_upper[0], sigma_lesser[0], screening[0],
            jnp.asarray(forward), jnp.asarray(inverse),
        )
        return result[None]

    spec = P("cuts", "energy", None, None, None)
    return jax.shard_map(
        shards, mesh=mesh, in_specs=(spec,) * 4, out_specs=spec, check_vma=False
    )
```

```python
import functools
import math

import jax
import jax.numpy as jnp
from jax import lax
from jax.experimental import pallas as pl
from jax.experimental.pallas import tpu as pltpu
from jax.sharding import PartitionSpec as P

LANES = 128
MESH = pl.DeviceIdType.MESH
F32 = jnp.float32
BF16 = jnp.bfloat16


def fill_tables(fwd_ref, inv_ref, groups, local):
    energies = groups * local
    period = 2 * energies
    rest = 2 * groups

    def index(shape, axis):
        return lax.broadcasted_iota(jnp.int32, shape, axis)

    def point(position):
        device = lax.div(lax.rem(position, rest), 2)
        return device * local + lax.div(position, rest), lax.rem(position, 2)

    def cosine(phase, quarters):
        phase = lax.rem(phase + quarters * (period // 4), period)
        return jnp.cos(phase.astype(F32) * (2.0 * math.pi / period))

    def split(table):
        high = table.astype(BF16)
        return high, (table - high.astype(F32)).astype(BF16)

    shape = (2 * period, period)
    energy, component = point(index(shape, 1))
    row = index(shape, 0)
    table = cosine(lax.rem(row, period) * energy, lax.div(row, period) + 4 - component)
    high, low = split(table)
    fwd_ref[...] = jnp.concatenate([high, low], axis=1)

    shape = (period, period)
    lag, component = point(index(shape, 0))
    table = cosine(lag * index(shape, 1), 4 - component) * (1.0 / (period * energies))
    high, low = split(table)
    inv_ref[...] = jnp.concatenate([high, high, low], axis=1)


def dot(left, right):
    return jnp.dot(left, right, preferred_element_type=F32)


def dot_t(left, right):
    return lax.dot_general(left, right, (((1,), (1,)), ((), ())), preferred_element_type=F32)


def times(lr, li, rr, ri):
    return dot(lr, rr) - dot(li, ri), dot(lr, ri) + dot(li, rr)


def times_adjoint(lr, li, rr, ri):
    return dot_t(lr, rr) + dot_t(li, ri), dot_t(li, rr) - dot_t(lr, ri)


def kernel(
    groups, slices, parts,
    gd_hbm, gu_hbm, s_hbm, w_hbm, out_hbm,
    fwd_ref, inv_ref,    gd, gu, sig, scr, snext, loan, own, lbuf, entries, xf, pf, pbuf, back, obuf,
    in_sem, z_send, z_recv, l_sem, a_send, a_recv, b_send, b_recv, o_sem,
):
    me = lax.axis_index("energy")
    cut = lax.axis_index("cuts")
    local, _, size, _ = gd.shape
    rows = size // groups
    part = rows // parts
    count = 2 * groups * local

    barrier = pltpu.get_barrier_semaphore()

    first = lax.rem(me, 2)
    partner = me + 1 - 2 * first
    last = local - 1

    def greet(k, carry):
        pl.semaphore_signal(
            barrier, inc=1, device_id={"energy": lax.rem(me + k, groups)}, device_id_type=MESH
        )
        return carry

    @pl.when(cut > 0)
    def _():
        for who in (me, partner):
            pl.semaphore_signal(
                barrier, inc=1, device_id={"energy": who, "cuts": cut - 1}, device_id_type=MESH
            )

    @pl.when(cut < slices - 1)
    def _():
        for who in (me, partner):
            pl.semaphore_signal(
                barrier, inc=1, device_id={"energy": who, "cuts": cut + 1}, device_id_type=MESH
            )

    lax.fori_loop(1, groups, greet, 0)

    loads = [
        pltpu.make_async_copy(source, target, in_sem.at[i])
        for i, (source, target) in enumerate(
            [(gd_hbm, gd), (s_hbm, sig), (gu_hbm, gu), (w_hbm, scr)]
        )
    ]
    loads[0].start()
    loads[1].start()

    edges = jnp.where(cut > 0, 1, 0) + jnp.where(cut < slices - 1, 1, 0)
    pl.semaphore_wait(barrier, groups - 1 + 2 * edges)

    def shift(j):
        return pltpu.make_async_remote_copy(
            src_ref=s_hbm.at[j], dst_ref=snext.at[j],
            send_sem=z_send.at[j], recv_sem=z_recv.at[j],
            device_id={"energy": me, "cuts": cut - 1}, device_id_type=MESH,
        )

    def lend():
        return pltpu.make_async_remote_copy(
            src_ref=s_hbm.at[last, 1 - first], dst_ref=loan,
            send_sem=l_sem.at[0], recv_sem=l_sem.at[1],
            device_id={"energy": partner, "cuts": cut}, device_id_type=MESH,
        )

    def shift_mine():
        return pltpu.make_async_remote_copy(
            src_ref=s_hbm.at[last, first], dst_ref=snext.at[last, first],
            send_sem=z_send.at[last], recv_sem=z_recv.at[last],
            device_id={"energy": me, "cuts": cut - 1}, device_id_type=MESH,
        )

    def shift_loan():
        return pltpu.make_async_remote_copy(
            src_ref=loan, dst_ref=snext.at[last, first],
            send_sem=z_send.at[local], recv_sem=z_recv.at[local],
            device_id={"energy": partner, "cuts": cut - 1}, device_id_type=MESH,
        )

    @pl.when(cut > 0)
    def _():
        lend().start()
        for j in range(last):
            shift(j).start()
        lend().wait_recv()

        @pl.when(first == 0)
        def _():
            shift_mine().start()
            shift_loan().start()

        @pl.when(first == 1)
        def _():
            shift_loan().start()
            shift_mine().start()

    for load in loads[2:]:
        load.start()
    fill_tables(fwd_ref, inv_ref, groups, local)
    loads[0].wait()
    loads[1].wait()

    def own_step(j, carry):
        tr, ti = times(gd[j, 0], gd[j, 1], sig[j, 0], sig[j, 1])
        lr, li = times_adjoint(tr.astype(BF16), ti.astype(BF16), gd[j, 0], gd[j, 1])
        own[j, 0] = lr
        own[j, 1] = li
        return carry

    lax.fori_loop(0, local, own_step, 0)
    for load in loads[2:]:
        load.wait()

    stretch = 2 * groups * part

    def take(j, h):
        landed = entries.at[j, h, pl.ds(0, groups - 1)]
        pltpu.make_async_copy(landed, landed, a_recv.at[j, h]).wait()
        wide = entries[j, h].astype(F32).reshape(stretch, size)
        for q in range(size // LANES):
            at = q * count * rows + h * count * part + j * stretch
            xf[pl.ds(at, stretch), :] = wide[:, q * LANES : (q + 1) * LANES]

    def each_part(body):
        lax.fori_loop(0, parts, lambda h, carry: (body(h), carry)[1], 0)

    def lesser_step(j, carry):
        @pl.when(cut < slices - 1)
        def _():
            @pl.when(j < last)
            def _():
                shift(j).wait_recv()

            @pl.when(j == last)
            def _():
                shift_mine().wait_recv()
                shift_loan().wait_recv()

            tr, ti = times(gu[j, 0], gu[j, 1], snext[j, 0], snext[j, 1])
            lr, li = times_adjoint(tr.astype(BF16), ti.astype(BF16), gu[j, 0], gu[j, 1])
            own[j, 0] += lr
            own[j, 1] += li

        for c in range(2):
            value = own[j, c].astype(BF16).reshape(groups, parts, part, size)
            for h in range(parts):
                lbuf[j, h, :, c] = value[:, h]

        def spread(h):
            def send(k, inner):
                to = lax.rem(me + k, groups)
                pltpu.make_async_remote_copy(
                    src_ref=lbuf.at[j, h, to], dst_ref=entries.at[j, h, me],
                    send_sem=a_send.at[j, h], recv_sem=a_recv.at[j, h],
                    device_id={"energy": to}, device_id_type=MESH,
                ).start()
                return inner

            lax.fori_loop(1, groups, send, 0)
            entries[j, h, me] = lbuf[j, h, me]

        each_part(spread)

        @pl.when(j > 0)
        def _():
            each_part(lambda h: take(j - 1, h))

        return carry

    lax.fori_loop(0, local, lesser_step, 0)

    period = count

    def part_step(h, outer):
        take(local - 1, h)

        def correlate(i, carry):
            at = h * count * part + i
            x = jnp.concatenate(
                [xf[pl.ds(q * count * rows + at, count, stride=part), :] for q in range(size // LANES)],
                axis=1,
            ).astype(BF16)
            spec = dot(fwd_ref[...], jnp.concatenate([x, x], axis=0))
            re, im = spec[:period], spec[period:]
            power = re * re + im * im
            high = power.astype(BF16)
            low = (power - high.astype(F32)).astype(BF16)
            lag = dot(inv_ref[...], jnp.concatenate([high, low, high], axis=0))
            for q in range(size // LANES):
                pf[pl.ds(q * count * rows + at, count, stride=part), :] = (
                    lag[:, q * LANES : (q + 1) * LANES]
                )
            return carry

        lax.fori_loop(0, part, correlate, 0, unroll=min(part, 4))

        def ship(j, carry):
            lags = jnp.concatenate(
                [
                    pf[pl.ds(q * count * rows + h * count * part + j * stretch, stretch), :]
                    for q in range(size // LANES)
                ],
                axis=1,
            )
            pbuf[h, j] = lags.reshape(groups, 2, part, size).astype(BF16)

            def send(k, inner):
                to = lax.rem(me + k, groups)
                pltpu.make_async_remote_copy(
                    src_ref=pbuf.at[h, j, to], dst_ref=back.at[j, h, me],
                    send_sem=b_send.at[h, j], recv_sem=b_recv.at[h, j],
                    device_id={"energy": to}, device_id_type=MESH,
                ).start()
                return inner

            lax.fori_loop(1, groups, send, 0)
            back[j, h, me] = pbuf[h, j, me]
            return carry

        lax.fori_loop(0, local, ship, 0)
        return outer

    lax.fori_loop(0, parts, part_step, 0)

    def result_step(j, carry):
        for h in range(parts):
            landed = back.at[j, h, pl.ds(0, groups - 1)]
            pltpu.make_async_copy(landed, landed, b_recv.at[h, j]).wait()
        pr, pi = (
            jnp.stack([back[j, h, :, c] for h in range(parts)], axis=1).reshape(size, size)
            for c in range(2)
        )
        tr, ti = times(scr[j, 0], scr[j, 1], pr, pi)
        lr, li = times_adjoint(tr.astype(BF16), ti.astype(BF16), scr[j, 0], scr[j, 1])
        obuf[j, 0] = lr.astype(BF16)
        obuf[j, 1] = li.astype(BF16)
        pltpu.make_async_copy(obuf.at[j], out_hbm.at[j], o_sem.at[j]).start()
        return carry

    lax.fori_loop(0, local, result_step, 0)

    @pl.when(cut > 0)
    def _():
        for j in range(last):
            shift(j).wait_send()
        shift_mine().wait_send()
        shift_loan().wait_send()
        lend().wait_send()

    for j in range(local):
        for h in range(parts):
            sent = lbuf.at[j, h, pl.ds(0, groups - 1)]
            pltpu.make_async_copy(sent, sent, a_send.at[j, h]).wait()
            sent = pbuf.at[h, j, pl.ds(0, groups - 1)]
            pltpu.make_async_copy(sent, sent, b_send.at[h, j]).wait()
        pltpu.make_async_copy(obuf.at[j], out_hbm.at[j], o_sem.at[j]).wait()


def solution(mesh):
    groups, slices = mesh.shape["energy"], mesh.shape["cuts"]

    def shards(green_diag, green_upper, sigma_lesser, screening):
        shape = green_diag.shape[1:]
        local, _, size, _ = shape
        rows = size // groups
        parts = max(1, rows // 8)
        part = rows // parts
        count = 2 * groups * local
        block = pltpu.VMEM(shape, BF16)
        dma = pltpu.SemaphoreType.DMA
        anywhere = pl.BlockSpec(memory_space=pltpu.HBM)
        result = pl.pallas_call(
            functools.partial(kernel, groups, slices, parts),
            out_shape=jax.ShapeDtypeStruct(shape, BF16),
            in_specs=[anywhere] * 4,
            out_specs=pl.BlockSpec(memory_space=pl.ANY),
            scratch_shapes=[
                pltpu.VMEM((2 * count, 2 * count), BF16),
                pltpu.VMEM((count, 3 * count), BF16),
                block, block, block, block, block,
                pltpu.VMEM(shape[2:], BF16),
                pltpu.VMEM(shape, F32),
                pltpu.VMEM((local, parts, groups, 2, part, size), BF16),
                pltpu.VMEM((local, parts, groups, 2, part, size), BF16),
                pltpu.VMEM((size // LANES * count * rows, LANES), F32),
                pltpu.VMEM((size // LANES * count * rows, LANES), F32),
                pltpu.VMEM((parts, local, groups, 2, part, size), BF16),
                pltpu.VMEM((local, parts, groups, 2, part, size), BF16),
                block,
                dma((4,)),
                dma((local + 1,)), dma((local + 1,)), dma((2,)),
                dma((local, parts)), dma((local, parts)),
                dma((parts, local)), dma((parts, local)),
                dma((local,)),
            ],
            compiler_params=pltpu.CompilerParams(
                collective_id=0, has_side_effects=True, vmem_limit_bytes=54525952
            ),
        )(
            green_diag[0], green_upper[0], sigma_lesser[0], screening[0]
        )
        return result[None]

    spec = P("cuts", "energy", None, None, None)
    return jax.shard_map(
        shards, mesh=mesh, in_specs=(spec,) * 4, out_specs=spec, check_vma=False
    )
```
